32 devices in a mesh: groups: 2 (over y), row: 4 (over z), col: 4 (over x, core).
Axes of the slice: x: 2, y: 2, z: 4, core: 2. Of those that a mesh axis runs over, the one named last changes fastest.
Arguments:
- block_tiles: bfloat16 [8, 4, 128, 128, 128], P(('groups', 'row'), 'col'), parts along dimension 0, may hold values from -0.125 to 0.125
- tile_row: int32 [8, 4, 128], P(('groups', 'row'), 'col'), parts along dimension 0, may hold values from 0 to 11, as said below
- tile_col: int32 [8, 4, 128], P(('groups', 'row'), 'col'), parts along dimension 0, may hold values from 0 to 11, as said below
- tile_count: int32 [8, 4], P(('groups', 'row'), 'col'), parts along dimension 0, may hold values from 1 to 128, as said below
- objective: float32 [12288], P(('groups', 'col')), parts along dimension 0, may hold values from -6 to 6
- upper_bound: float32 [12288], P(('groups', 'col')), parts along dimension 0, may hold values from 0.5 to 4
- power_caps: float32 [64, 6144], P('groups', 'row'), parts along dimension 0, may hold values from -6 to 6
- primal_start: float32 [64, 6144], P('groups', 'col'), parts along dimension 0, may hold values from 0 to 0.5
- dual_start: float32 [64, 6144], P('groups', 'row'), parts along dimension 0, may hold values from 0 to 1
Outputs:
- primal_final: float32 [64, 6144], P('groups', 'col'), parts along dimension 0
- dual_final: float32 [64, 6144], P('groups', 'row'), parts along dimension 0
The draws below stay inside these ranges and needn't reach their ends.
There are 2 independent parts, one for each index of `groups`. The reference program is written for one: setup_inputs(seed, part) draws one part's arguments, and reference() takes and returns one part's arrays. A program takes and returns all parts, laid end to end along the dimension named above; each array names one. Nothing has to cross between parts.
Inputs may be any that keep to these rules, and one draw needn't show every extreme that they name: `tile_row`: constraint block of a slot, local to its row index. `tile_col`: variable block of a slot, local to its col index; the slots of one device name distinct pairs of (tile_row, tile_col). `tile_count`: some device of every draw has all 128 slots live; the busiest devices hold about three times the mean.
All inputs are finite; a program needn't handle non-finite values.
Results may differ from the reference program's by a relative error of at most 0.0011.
Values sent between devices are 32-bit elements; how exact they have to be, the bound alone decides.
A program may use at most 64 MiB of HBM per device.

```python
import math
import jax
import jax.numpy as jnp
from jax import lax

B = 128
S = 32
RB_DEV = 12
CB_DEV = 12
TILES = 128
ITERS = 6
NCON = 6144
NVAR = 6144
N_ROW = 4
N_COL = 4


def slot_positions(key):
    row_devs = NCON // (RB_DEV * B)
    col_devs = NVAR // (CB_DEV * B)
    subkeys = jax.random.split(jax.random.fold_in(key, 23), row_devs * col_devs)
    orders = jax.vmap(lambda single: jax.random.permutation(single, RB_DEV * CB_DEV))(subkeys)
    chosen = orders[:, :TILES].astype(jnp.int32).reshape(row_devs, col_devs, TILES)
    return chosen


def draw_tile_row(key, part):
    return (slot_positions(key) // CB_DEV).astype(jnp.int32)


def draw_tile_col(key, part):
    return (slot_positions(key) % CB_DEV).astype(jnp.int32)


def draw_tile_count(key, part):
    row_devs = NCON // (RB_DEV * B)
    col_devs = NVAR // (CB_DEV * B)
    first, second, third, fourth = jax.random.split(jax.random.fold_in(key, 41), 4)
    shape_two = (row_devs, col_devs)
    lower_count = jax.random.randint(first, shape_two, max(1, TILES // 6), max(1, TILES // 3) + 1)
    higher_count = jax.random.randint(second, shape_two, max(1, TILES // 2), TILES + 1)
    busy_flag = jax.random.randint(third, shape_two, 0, 8) == 0
    counts = jnp.where(busy_flag, higher_count, lower_count)
    full_device = jax.random.randint(fourth, (), 0, row_devs * col_devs)
    flat_index = jnp.arange(row_devs * col_devs, dtype=jnp.int32).reshape(shape_two)
    counts = jnp.where(flat_index == full_device, TILES, counts)
    return counts.astype(jnp.int32)


def steps_of(own_key, dims, cuts, low, high):
    loudness = 1.0
    for position, blocks in cuts:
        steps = jax.random.uniform(jax.random.fold_in(jax.random.fold_in(own_key, 6), position), (blocks,), jnp.float32, low / len(cuts), high / len(cuts))
        loudness = loudness * jnp.repeat(jnp.exp(steps), dims[position] // blocks).reshape((-1,) + (1,) * (len(dims) - 1 - position))
    return loudness


def centred(stream_key, extent, deviation, limit, cuts=(), kind=jnp.bfloat16):
    drawn = jax.random.normal(stream_key, extent, jnp.float32) * deviation
    if len(cuts) > 0:
        drawn = steps_of(stream_key, extent, cuts, -0.22, 0.18) * drawn
    return jnp.clip(drawn, min=-limit, max=limit).astype(kind)


def setup_inputs(seed: int = 0, part: int = 0) -> dict:
    key_of = jax.random.split(jax.random.key(seed), 10)
    part_keys = jax.random.split(jax.random.fold_in(key_of[9], part), 10)
    return {
        "block_tiles": centred(part_keys[0], (N_ROW, N_COL, TILES, B, B), (B * CB_DEV * N_COL // 3) ** -0.5, 0.125, ((0, 4), (1, 4))),
        "tile_row": draw_tile_row(jax.random.fold_in(jax.random.fold_in(key_of[9], part), 71), part),
        "tile_col": draw_tile_col(jax.random.fold_in(jax.random.fold_in(key_of[9], part), 71), part),
        "tile_count": draw_tile_count(jax.random.fold_in(jax.random.fold_in(key_of[9], part), 71), part),
        "objective": centred(part_keys[4], (NVAR,), 1.0, 6.0, ((0, 4),), jnp.float32),
        "upper_bound": jnp.clip(jnp.exp(math.log(4.0) - 2.0794415 * jax.random.uniform(part_keys[5], (NVAR,), jnp.float32) ** steps_of(part_keys[5], (NVAR,), ((0, 4),), -0.2, 0.2)), 0.5, 4.0),
        "power_caps": centred(part_keys[6], (S, NCON), 1.0, 6.0, ((1, 4),), jnp.float32),
        "primal_start": jnp.clip(0.5 * jax.random.uniform(part_keys[7], (S, NVAR), jnp.float32) ** steps_of(part_keys[7], (S, NVAR), ((1, 4),), -0.2, 0.2), 0.0, 0.5),
        "dual_start": jnp.clip(1.0 * jax.random.uniform(part_keys[8], (S, NCON), jnp.float32) ** steps_of(part_keys[8], (S, NCON), ((1, 4),), -0.2, 0.2), 0.0, 1.0),
    }


PRIMAL_STEP = 0.5
DUAL_STEP = 0.2


def live_table(tile_count):
    slots = jnp.arange(TILES, dtype=jnp.int32)
    return (slots[None, None, :] < tile_count[:, :, None]).astype(jnp.float32)


def adjoint_product(dual_low, block_tiles, tile_row, tile_col, live_slots):
    dual_four = dual_low.astype(jnp.float32).reshape(S, N_ROW, RB_DEV, B)
    columns = jnp.arange(CB_DEV, dtype=jnp.int32)

    def one_row(totals, row_index):
        dual_rows = dual_four[:, row_index]
        selected = dual_rows[:, tile_row[row_index]]
        product = jnp.einsum("sctb,ctbk->sctk", selected, block_tiles[row_index].astype(jnp.float32), precision=lax.Precision.HIGHEST)
        product = product * live_slots[row_index][None, :, :, None]
        onehot = (tile_col[row_index][:, :, None] == columns[None, None, :]).astype(jnp.float32)
        pieces = jnp.einsum("sctk,ctj->scjk", product, onehot, precision=lax.Precision.HIGHEST)
        return totals + pieces, None

    totals, _ = lax.scan(one_row, jnp.zeros((S, N_COL, CB_DEV, B), jnp.float32), jnp.arange(N_ROW, dtype=jnp.int32))
    return totals.reshape(S, NVAR)


def forward_product(extrap, block_tiles, tile_row, tile_col, live_slots):
    primal_four = extrap.astype(jnp.float32).reshape(S, N_COL, CB_DEV, B)
    col_index = jnp.arange(N_COL, dtype=jnp.int32)
    rows_local = jnp.arange(RB_DEV, dtype=jnp.int32)

    def one_row(carry_value, row_index):
        selected = primal_four[:, col_index[:, None], tile_col[row_index]]
        product = jnp.einsum("sctk,ctbk->sctb", selected, block_tiles[row_index].astype(jnp.float32), precision=lax.Precision.HIGHEST)
        product = product * live_slots[row_index][None, :, :, None]
        onehot = (tile_row[row_index][:, :, None] == rows_local[None, None, :]).astype(jnp.float32)
        pieces = jnp.einsum("sctb,ctj->sjb", product, onehot, precision=lax.Precision.HIGHEST)
        return carry_value, pieces

    _, stacked = lax.scan(one_row, jnp.zeros((), jnp.float32), jnp.arange(N_ROW, dtype=jnp.int32))
    return jnp.transpose(stacked, (1, 0, 2, 3)).reshape(S, NCON)


def reference(block_tiles, tile_row, tile_col, tile_count, objective, upper_bound, power_caps, primal_start, dual_start):
    live_slots = live_table(tile_count)
    primal = primal_start
    dual = dual_start
    for iteration in range(ITERS):
        dual_low = lax.optimization_barrier(dual.astype(jnp.bfloat16))
        adjoint = adjoint_product(dual_low, block_tiles, tile_row, tile_col, live_slots)
        primal_next = jnp.minimum(jnp.maximum(primal - PRIMAL_STEP * (objective[None, :] - adjoint), 0.0), upper_bound[None, :])
        extrap = lax.optimization_barrier((2.0 * primal_next - primal).astype(jnp.bfloat16))
        forward = forward_product(extrap, block_tiles, tile_row, tile_col, live_slots)
        dual = jnp.maximum(dual + DUAL_STEP * (power_caps - forward), 0.0)
        primal = primal_next
    return primal, dual
```

```python
import functools

import jax
import jax.numpy as jnp
from jax import lax
from jax.experimental import pallas as pl
from jax.experimental.pallas import tpu as pltpu
from jax.sharding import PartitionSpec as P

ITERS = 6


PRIMAL_STEP = 0.5
DUAL_STEP = 0.2

TILE_STEP = 16
MESH = pl.DeviceIdType.MESH


def build_kernel(step_slots, rows_ref, cols_ref, count_ref, tiles_ref, k_ref, kt_ref):
    block = tiles_ref.shape[1]
    k_per = k_ref.shape[2] // block
    kt_per = kt_ref.shape[2] // block
    step = pl.program_id(0)

    @pl.when(step == 0)
    def _():
        k_ref[...] = jnp.zeros_like(k_ref)
        kt_ref[...] = jnp.zeros_like(kt_ref)

    for i in range(step_slots):
        slot = step * step_slots + i

        @pl.when(slot < count_ref[0])
        def _():
            row = rows_ref[slot]
            col = cols_ref[slot]
            tile = tiles_ref[i]
            row_at = pl.multiple_of(row * block, block)
            col_at = pl.multiple_of(col * block, block)
            k_in = pl.multiple_of(lax.rem(col, k_per) * block, block)
            kt_in = pl.multiple_of(lax.rem(row, kt_per) * block, block)
            k_ref[lax.div(col, k_per), pl.ds(row_at, block), pl.ds(k_in, block)] = tile
            kt_ref[lax.div(row, kt_per), pl.ds(col_at, block), pl.ds(kt_in, block)] = tile.T


def build_dense(tiles, rows, cols, count, cons, nvar, k_chunks, kt_chunks):
    slots, block = tiles.shape[0], tiles.shape[1]
    step_slots = TILE_STEP if slots % TILE_STEP == 0 else 1
    k_shape = (k_chunks, cons, nvar // k_chunks)
    kt_shape = (kt_chunks, nvar, cons // kt_chunks)
    return pl.pallas_call(
        functools.partial(build_kernel, step_slots),
        out_shape=(
            jax.ShapeDtypeStruct(k_shape, tiles.dtype),
            jax.ShapeDtypeStruct(kt_shape, tiles.dtype),
        ),
        grid_spec=pltpu.PrefetchScalarGridSpec(
            num_scalar_prefetch=3,
            grid=(slots // step_slots,),
            in_specs=[pl.BlockSpec((step_slots, block, block), lambda t, *_: (t, 0, 0))],
            out_specs=(
                pl.BlockSpec(k_shape, lambda t, *_: (0, 0, 0)),
                pl.BlockSpec(kt_shape, lambda t, *_: (0, 0, 0)),
            ),
        ),
        compiler_params=pltpu.CompilerParams(vmem_limit_bytes=40 << 20),
        name="build_dense",
    )(rows, cols, count, tiles)


def pdhg_kernel(
    iters,
    k_ref,
    kt_ref,
    obj_ref,
    ub_ref,
    caps_ref,
    p0_ref,
    d0_ref,
    p_out,
    d_out,
    primal,
    primal_new,
    dual,
    adj_part,
    adj_got,
    fwd_part,
    fwd_got,
    extrap_low,
    dual_low,
    adj_send,
    adj_recv,
    pri_send,
    pri_recv,
    fwd_send,
    fwd_recv,
    dua_send,
    dua_recv,
):
    halves, n_row, rows_half, v_chunk = primal.shape
    _, n_col, _, c_chunk = dual.shape
    r = lax.axis_index("row")
    c = lax.axis_index("col")

    barrier = pltpu.get_barrier_semaphore()
    for k in range(1, n_row):
        pl.semaphore_signal(
            barrier, inc=1, device_id={"row": lax.rem(r + k, n_row)}, device_id_type=MESH
        )
    for k in range(1, n_col):
        pl.semaphore_signal(
            barrier, inc=1, device_id={"col": lax.rem(c + k, n_col)}, device_id_type=MESH
        )

    v_own = pl.ds(pl.multiple_of(r * v_chunk, 128), v_chunk)
    c_own = pl.ds(pl.multiple_of(c * c_chunk, 128), c_chunk)

    def rows_of(h):
        return pl.ds(h * rows_half, rows_half)

    for h in range(halves):
        for j in range(n_row):
            primal[h, j] = p0_ref[rows_of(h), pl.ds(j * v_chunk, v_chunk)]
        for j in range(n_col):
            dual[h, j] = d0_ref[rows_of(h), pl.ds(j * c_chunk, c_chunk)]

    def spread(axis, me, count, k, src, dst, send, recv):
        return pltpu.make_async_remote_copy(
            src_ref=src,
            dst_ref=dst,
            send_sem=send,
            recv_sem=recv,
            device_id={axis: lax.rem(me + k, count)},
            device_id_type=MESH,
        )

    def adj_copy(h, k):
        dest = lax.rem(r + k, n_row)
        return spread(
            "row", r, n_row, k, adj_part.at[h, dest], adj_got.at[h, k],
            adj_send.at[h, k], adj_recv.at[h, k],
        )

    def pri_copy(h, k):
        return spread(
            "row", r, n_row, k, primal_new.at[h, r], primal_new.at[h, r],
            pri_send.at[h, k], pri_recv.at[h, k],
        )

    def fwd_copy(h, k):
        dest = lax.rem(c + k, n_col)
        return spread(
            "col", c, n_col, k, fwd_part.at[h, dest], fwd_got.at[h, k],
            fwd_send.at[h, k], fwd_recv.at[h, k],
        )

    def dua_copy(h, k):
        return spread(
            "col", c, n_col, k, dual.at[h, c], dual.at[h, c],
            dua_send.at[h, k], dua_recv.at[h, k],
        )

    def adjoint_start(h, first):
        if not first:
            for k in range(1, n_col):
                dua_copy(h, k).wait()
        for j in range(n_col):
            dual_low[h, :, j * c_chunk : (j + 1) * c_chunk] = dual[h, j].astype(jnp.bfloat16)
        for k in list(range(1, n_row)) + [0]:
            dest = lax.rem(r + k, n_row)
            adj_part[h, dest] = jnp.dot(
                dual_low[h], k_ref[dest], preferred_element_type=jnp.float32
            )
            if k:
                adj_copy(h, k).start()

    def primal_step(h):
        adjoint = adj_part[h, r]
        for k in range(1, n_row):
            adj_copy(h, k).wait()
            adjoint = adjoint + adj_got[h, k]
        primal_new[h, r] = jnp.minimum(
            jnp.maximum(primal[h, r] - PRIMAL_STEP * (obj_ref[:, v_own] - adjoint), 0.0),
            ub_ref[:, v_own],
        )
        for k in range(1, n_row):
            pri_copy(h, k).start()

    def forward_start(h):
        for k in range(1, n_row):
            pri_copy(h, k).wait()
        for j in range(n_row):
            new = primal_new[h, j]
            extrap_low[h, :, j * v_chunk : (j + 1) * v_chunk] = (
                2.0 * new - primal[h, j]
            ).astype(jnp.bfloat16)
            primal[h, j] = new
        for k in list(range(1, n_col)) + [0]:
            dest = lax.rem(c + k, n_col)
            fwd_part[h, dest] = jnp.dot(
                extrap_low[h], kt_ref[dest], preferred_element_type=jnp.float32
            )
            if k:
                fwd_copy(h, k).start()

    def dual_step(h):
        forward = fwd_part[h, c]
        for k in range(1, n_col):
            fwd_copy(h, k).wait()
            forward = forward + fwd_got[h, k]
        dual[h, c] = jnp.maximum(
            dual[h, c] + DUAL_STEP * (caps_ref[rows_of(h), c_own] - forward), 0.0
        )
        for k in range(1, n_col):
            dua_copy(h, k).start()

    pl.semaphore_wait(barrier, n_row + n_col - 2)

    if halves == 1:
        adjoint_start(0, True)
        primal_step(0)
        forward_start(0)
        dual_step(0)

        def body(_, carry):
            adjoint_start(0, False)
            primal_step(0)
            forward_start(0)
            dual_step(0)
            return carry

        lax.fori_loop(1, iters, body, 0)
    else:
        adjoint_start(0, True)
        primal_step(0)
        adjoint_start(1, True)
        forward_start(0)
        primal_step(1)
        dual_step(0)

        def body(_, carry):
            adjoint_start(0, False)
            forward_start(1)
            primal_step(0)
            dual_step(1)
            adjoint_start(1, False)
            forward_start(0)
            primal_step(1)
            dual_step(0)
            return carry

        lax.fori_loop(1, iters, body, 0)
        forward_start(1)
        dual_step(1)

    for h in range(halves):
        for j in range(n_row):
            p_out[rows_of(h), pl.ds(j * v_chunk, v_chunk)] = primal[h, j]
        for k in range(1, n_col):
            dua_copy(h, k).wait()
        for j in range(n_col):
            d_out[rows_of(h), pl.ds(j * c_chunk, c_chunk)] = dual[h, j]


def pdhg(dense, dense_t, objective, upper_bound, power_caps, primal_start, dual_start):
    n_row, cons, v_chunk = dense.shape
    n_col, nvar, c_chunk = dense_t.shape
    scenarios = primal_start.shape[0]
    halves = 2 if scenarios % 32 == 0 else 1
    rows_half = scenarios // halves
    vmem = pl.BlockSpec(memory_space=pltpu.VMEM)
    f32 = jnp.float32
    row_shape = (halves, n_row, rows_half, v_chunk)
    col_shape = (halves, n_col, rows_half, c_chunk)
    row_sem = pltpu.SemaphoreType.DMA((halves, n_row))
    col_sem = pltpu.SemaphoreType.DMA((halves, n_col))
    return pl.pallas_call(
        functools.partial(pdhg_kernel, ITERS),
        out_shape=(
            jax.ShapeDtypeStruct((scenarios, nvar), f32),
            jax.ShapeDtypeStruct((scenarios, cons), f32),
        ),
        in_specs=[vmem] * 7,
        out_specs=(vmem, vmem),
        scratch_shapes=[
            pltpu.VMEM(row_shape, f32),
            pltpu.VMEM(row_shape, f32),
            pltpu.VMEM(col_shape, f32),
            pltpu.VMEM(row_shape, f32),
            pltpu.VMEM(row_shape, f32),
            pltpu.VMEM(col_shape, f32),
            pltpu.VMEM(col_shape, f32),
            pltpu.VMEM((halves, rows_half, nvar), jnp.bfloat16),
            pltpu.VMEM((halves, rows_half, cons), jnp.bfloat16),
            row_sem,
            row_sem,
            row_sem,
            row_sem,
            col_sem,
            col_sem,
            col_sem,
            col_sem,
        ],
        compiler_params=pltpu.CompilerParams(
            collective_id=0, has_side_effects=True, vmem_limit_bytes=40 << 20
        ),
        name="pdhg",
    )(
        dense,
        dense_t,
        objective[None, :],
        upper_bound[None, :],
        power_caps,
        primal_start,
        dual_start,
    )


def pdhg_summed(dense, dense_t, objective, upper_bound, power_caps, primal, dual):
    for _ in range(ITERS):
        part = jnp.dot(dual.astype(jnp.bfloat16), dense[0], preferred_element_type=jnp.float32)
        adjoint = lax.psum(part, "row")
        new = jnp.minimum(
            jnp.maximum(primal - PRIMAL_STEP * (objective[None, :] - adjoint), 0.0),
            upper_bound[None, :],
        )
        extrap = (2.0 * new - primal).astype(jnp.bfloat16)
        part = jnp.dot(extrap, dense_t[0], preferred_element_type=jnp.float32)
        forward = lax.psum(part, "col")
        dual = jnp.maximum(dual + DUAL_STEP * (power_caps - forward), 0.0)
        primal = new
    return primal, dual


def per_device(
    n_row,
    n_col,
    block_tiles,
    tile_row,
    tile_col,
    tile_count,
    objective,
    upper_bound,
    power_caps,
    primal_start,
    dual_start,
):
    block = block_tiles.shape[-1]
    cons = dual_start.shape[1]
    nvar = primal_start.shape[1]
    even = (nvar // block) % n_row == 0 and (cons // block) % n_col == 0
    dense, dense_t = build_dense(
        block_tiles[0, 0],
        tile_row[0, 0],
        tile_col[0, 0],
        tile_count[0],
        cons,
        nvar,
        n_row if even else 1,
        n_col if even else 1,
    )
    steps = pdhg if even else pdhg_summed
    return steps(dense, dense_t, objective, upper_bound, power_caps, primal_start, dual_start)


def solution(mesh):
    return jax.shard_map(
        functools.partial(per_device, mesh.shape["row"], mesh.shape["col"]),
        mesh=mesh,
        in_specs=(
            P(("groups", "row"), "col", None, None, None),
            P(("groups", "row"), "col", None),
            P(("groups", "row"), "col", None),
            P(("groups", "row"), "col"),
            P(("groups", "col")),
            P(("groups", "col")),
            P("groups", "row"),
            P("groups", "col"),
            P("groups", "row"),
        ),
        out_specs=(P("groups", "col"), P("groups", "row")),
        check_vma=False,
    )
```

```python
import functools

import jax
import jax.numpy as jnp
from jax import lax
from jax.experimental import pallas as pl
from jax.experimental.pallas import tpu as pltpu
from jax.sharding import PartitionSpec as P

ITERS = 6


PRIMAL_STEP = 0.5
DUAL_STEP = 0.2

TILE_STEP = 16
GROUPS = 2
PIECES = 2
MESH = pl.DeviceIdType.MESH


def build_kernel(step_slots, rows_ref, cols_ref, count_ref, tiles_ref, k_ref):
    block = tiles_ref.shape[1]
    step = pl.program_id(0)

    @pl.when(step == 0)
    def _():
        k_ref[...] = jnp.zeros_like(k_ref)

    for i in range(step_slots):
        slot = step * step_slots + i

        @pl.when(slot < count_ref[0])
        def _():
            row_at = pl.multiple_of(rows_ref[slot] * block, block)
            col_at = pl.multiple_of(cols_ref[slot] * block, block)
            k_ref[pl.ds(row_at, block), pl.ds(col_at, block)] = tiles_ref[i]


def build_dense(tiles, rows, cols, count, cons, nvar):
    slots, block = tiles.shape[0], tiles.shape[1]
    step_slots = TILE_STEP if slots % TILE_STEP == 0 else 1
    return pl.pallas_call(
        functools.partial(build_kernel, step_slots),
        out_shape=jax.ShapeDtypeStruct((cons, nvar), tiles.dtype),
        grid_spec=pltpu.PrefetchScalarGridSpec(
            num_scalar_prefetch=3,
            grid=(slots // step_slots,),
            in_specs=[pl.BlockSpec((step_slots, block, block), lambda t, *_: (t, 0, 0))],
            out_specs=pl.BlockSpec((cons, nvar), lambda t, *_: (0, 0)),
        ),
        compiler_params=pltpu.CompilerParams(vmem_limit_bytes=40 << 20),
        name="build_dense",
    )(rows, cols, count, tiles)


def partner(me, stage):
    low = 1 << stage
    bit = lax.rem(lax.div(me, low), 2)
    return me + low - 2 * low * bit


def pdhg_kernel(
    iters,
    block,
    k_ref,
    obj_ref,
    ub_ref,
    caps_ref,
    p0_ref,
    d0_ref,
    primal,
    dual,
    kt_ref,
    adj_sum,
    adj_got,
    fwd_sum,
    fwd_got,
    adj_send,
    adj_recv,
    fwd_send,
    fwd_recv,
):
    row_stages, groups, pieces, rows, v_piece = adj_sum.shape
    col_stages, _, _, _, c_piece = fwd_sum.shape
    cons, nvar = k_ref.shape
    r = lax.axis_index("row")
    c = lax.axis_index("col")

    barrier = pltpu.get_barrier_semaphore()
    for s in range(row_stages):
        pl.semaphore_signal(
            barrier, inc=1, device_id={"row": partner(r, s)}, device_id_type=MESH
        )
    for s in range(col_stages):
        pl.semaphore_signal(
            barrier, inc=1, device_id={"col": partner(c, s)}, device_id_type=MESH
        )

    primal[...] = p0_ref[...]
    dual[...] = d0_ref[...]

    def rows_of(g):
        return pl.ds(g * rows, rows)

    def adj_copy(s, g, n, parity):
        return pltpu.make_async_remote_copy(
            src_ref=adj_sum.at[s, g, n],
            dst_ref=adj_got.at[parity, s, g, n],
            send_sem=adj_send.at[s, g, n],
            recv_sem=adj_recv.at[parity, s, g, n],
            device_id={"row": partner(r, s)},
            device_id_type=MESH,
        )

    def fwd_copy(s, g, n, parity):
        return pltpu.make_async_remote_copy(
            src_ref=fwd_sum.at[s, g, n],
            dst_ref=fwd_got.at[parity, s, g, n],
            send_sem=fwd_send.at[s, g, n],
            recv_sem=fwd_recv.at[parity, s, g, n],
            device_id={"col": partner(c, s)},
            device_id_type=MESH,
        )

    def exchange(copy, total, got, stages, parity, first, finish):
        for s in range(stages):
            for g in range(groups):
                for n in range(pieces):
                    copy(s, g, n, parity).wait_recv()
                    value = total[s, g, n] + got[parity, s, g, n]
                    if s + 1 < stages:
                        if not first:
                            copy(s + 1, g, n, parity).wait_send()
                        total[s + 1, g, n] = value
                        copy(s + 1, g, n, parity).start()
                    else:
                        finish(g, n, value)
                if s + 1 == stages:
                    finish(g, None, None)

    def products(copy, total, width, lhs, weights, g, parity, first):
        for n in range(pieces):
            if not first:
                copy(0, g, n, parity).wait_send()
            total[0, g, n] = jnp.dot(
                lhs, weights[:, n * width : (n + 1) * width], preferred_element_type=jnp.float32
            )
            copy(0, g, n, parity).start()

    def adjoint_start(g, parity, first):
        low = dual[rows_of(g), :].astype(jnp.bfloat16)
        products(adj_copy, adj_sum, v_piece, low, k_ref, g, parity, first)

    def iteration(parity, first, last):
        extrap = [[None] * pieces for _ in range(groups)]

        def primal_step(g, n, adjoint):
            if n is None:
                low = jnp.concatenate(extrap[g], axis=1)
                products(fwd_copy, fwd_sum, c_piece, low, kt_ref, g, parity, first)
                return
            lanes = pl.ds(n * v_piece, v_piece)
            old = primal[rows_of(g), lanes]
            new = jnp.minimum(
                jnp.maximum(old - PRIMAL_STEP * (obj_ref[:, lanes] - adjoint), 0.0),
                ub_ref[:, lanes],
            )
            primal[rows_of(g), lanes] = new
            extrap[g][n] = (2.0 * new - old).astype(jnp.bfloat16)

        def dual_step(g, n, forward):
            if n is None:
                if not last:
                    adjoint_start(g, 1 - parity, False)
                return
            lanes = pl.ds(n * c_piece, c_piece)
            dual[rows_of(g), lanes] = jnp.maximum(
                dual[rows_of(g), lanes]
                + DUAL_STEP * (caps_ref[rows_of(g), lanes] - forward),
                0.0,
            )

        exchange(adj_copy, adj_sum, adj_got, row_stages, parity, first, primal_step)
        exchange(fwd_copy, fwd_sum, fwd_got, col_stages, parity, first, dual_step)

    pl.semaphore_wait(barrier, row_stages + col_stages)

    for g in range(groups):
        adjoint_start(g, 0, True)

    def transpose_rows(i, carry):
        at = pl.multiple_of(i * block, block)
        for j in range(nvar // block):
            kt_ref[j * block : (j + 1) * block, pl.ds(at, block)] = k_ref[
                pl.ds(at, block), j * block : (j + 1) * block
            ].T
        return carry

    lax.fori_loop(0, cons // block, transpose_rows, 0)

    iteration(0, True, False)

    def body(i, carry):
        iteration(lax.rem(i, 2), False, False)
        return carry

    lax.fori_loop(1, iters - 1, body, 0)
    iteration((iters - 1) % 2, False, True)

    for g in range(groups):
        for n in range(pieces):
            for s in range(row_stages):
                adj_copy(s, g, n, 0).wait_send()
            for s in range(col_stages):
                fwd_copy(s, g, n, 0).wait_send()


def pdhg(block, n_row, n_col, dense, objective, upper_bound, power_caps, primal_start, dual_start):
    cons, nvar = dense.shape
    scenarios = primal_start.shape[0]
    groups, pieces = GROUPS, PIECES
    row_stages, col_stages = n_row.bit_length() - 1, n_col.bit_length() - 1
    assert (1 << row_stages, 1 << col_stages) == (n_row, n_col)
    rows = scenarios // groups
    vmem = pl.BlockSpec(memory_space=pltpu.VMEM)
    f32 = jnp.float32
    adj = (row_stages, groups, pieces)
    fwd = (col_stages, groups, pieces)
    v_piece, c_piece = nvar // pieces, cons // pieces
    return pl.pallas_call(
        functools.partial(pdhg_kernel, ITERS, block),
        out_shape=(
            jax.ShapeDtypeStruct((scenarios, nvar), f32),
            jax.ShapeDtypeStruct((scenarios, cons), f32),
        ),
        in_specs=[vmem] * 6,
        out_specs=(vmem, vmem),
        scratch_shapes=[
            pltpu.VMEM((nvar, cons), dense.dtype),
            pltpu.VMEM((*adj, rows, v_piece), f32),
            pltpu.VMEM((2, *adj, rows, v_piece), f32),
            pltpu.VMEM((*fwd, rows, c_piece), f32),
            pltpu.VMEM((2, *fwd, rows, c_piece), f32),
            pltpu.SemaphoreType.DMA(adj),
            pltpu.SemaphoreType.DMA((2, *adj)),
            pltpu.SemaphoreType.DMA(fwd),
            pltpu.SemaphoreType.DMA((2, *fwd)),
        ],
        compiler_params=pltpu.CompilerParams(
            collective_id=0, has_side_effects=True, vmem_limit_bytes=40 << 20
        ),
        name="pdhg",
    )(
        dense,
        objective[None, :],
        upper_bound[None, :],
        power_caps,
        primal_start,
        dual_start,
    )


def per_device(
    n_row,
    n_col,
    block_tiles,
    tile_row,
    tile_col,
    tile_count,
    objective,
    upper_bound,
    power_caps,
    primal_start,
    dual_start,
):
    dense = build_dense(
        block_tiles[0, 0],
        tile_row[0, 0],
        tile_col[0, 0],
        tile_count[0],
        dual_start.shape[1],
        primal_start.shape[1],
    )
    return pdhg(
        block_tiles.shape[-1],
        n_row,
        n_col,
        dense,
        objective,
        upper_bound,
        power_caps,
        primal_start,
        dual_start,
    )


def solution(mesh):
    return jax.shard_map(
        functools.partial(per_device, mesh.shape["row"], mesh.shape["col"]),
        mesh=mesh,
        in_specs=(
            P(("groups", "row"), "col", None, None, None),
            P(("groups", "row"), "col", None),
            P(("groups", "row"), "col", None),
            P(("groups", "row"), "col"),
            P(("groups", "col")),
            P(("groups", "col")),
            P("groups", "row"),
            P("groups", "col"),
            P("groups", "row"),
        ),
        out_specs=(P("groups", "col"), P("groups", "row")),
        check_vma=False,
    )
```

```python
import functools

import jax
import jax.numpy as jnp
from jax import lax
from jax.experimental import pallas as pl
from jax.experimental.pallas import tpu as pltpu
from jax.sharding import PartitionSpec as P

ITERS = 6


PRIMAL_STEP = 0.5
DUAL_STEP = 0.2

TILE_STEP = 16
MESH = pl.DeviceIdType.MESH


def build_kernel(step_slots, rows_ref, cols_ref, count_ref, tiles_ref, k_ref):
    block = tiles_ref.shape[1]
    k_per = k_ref.shape[2] // block
    step = pl.program_id(0)

    @pl.when(step == 0)
    def _():
        k_ref[...] = jnp.zeros_like(k_ref)

    for i in range(step_slots):
        slot = step * step_slots + i

        @pl.when(slot < count_ref[0])
        def _():
            row = rows_ref[slot]
            col = cols_ref[slot]
            row_at = pl.multiple_of(row * block, block)
            k_in = pl.multiple_of(lax.rem(col, k_per) * block, block)
            k_ref[lax.div(col, k_per), pl.ds(row_at, block), pl.ds(k_in, block)] = tiles_ref[i]


def build_dense(tiles, rows, cols, count, cons, nvar, k_chunks):
    slots, block = tiles.shape[0], tiles.shape[1]
    step_slots = TILE_STEP if slots % TILE_STEP == 0 else 1
    k_shape = (k_chunks, cons, nvar // k_chunks)
    return pl.pallas_call(
        functools.partial(build_kernel, step_slots),
        out_shape=jax.ShapeDtypeStruct(k_shape, tiles.dtype),
        grid_spec=pltpu.PrefetchScalarGridSpec(
            num_scalar_prefetch=3,
            grid=(slots // step_slots,),
            in_specs=[pl.BlockSpec((step_slots, block, block), lambda t, *_: (t, 0, 0))],
            out_specs=pl.BlockSpec(k_shape, lambda t, *_: (0, 0, 0)),
        ),
        compiler_params=pltpu.CompilerParams(vmem_limit_bytes=40 << 20),
        name="build_dense",
    )(rows, cols, count, tiles)


def pdhg_kernel(
    iters,
    block,
    k_ref,
    obj_ref,
    ub_ref,
    caps_ref,
    p0_ref,
    d0_ref,
    p_out,
    d_out,
    kt_ref,
    primal,
    primal_new,
    dual,
    adj_part,
    adj_got,
    fwd_part,
    fwd_got,
    extrap_low,
    dual_low,
    adj_send,
    adj_recv,
    pri_send,
    pri_recv,
    fwd_send,
    fwd_recv,
    dua_send,
    dua_recv,
):
    halves, n_row, rows_half, v_chunk = primal.shape
    _, n_col, _, c_chunk = dual.shape
    r = lax.axis_index("row")
    c = lax.axis_index("col")

    barrier = pltpu.get_barrier_semaphore()
    for k in range(1, n_row):
        pl.semaphore_signal(
            barrier, inc=1, device_id={"row": lax.rem(r + k, n_row)}, device_id_type=MESH
        )
    for k in range(1, n_col):
        pl.semaphore_signal(
            barrier, inc=1, device_id={"col": lax.rem(c + k, n_col)}, device_id_type=MESH
        )

    v_own = pl.ds(pl.multiple_of(r * v_chunk, 128), v_chunk)
    c_own = pl.ds(pl.multiple_of(c * c_chunk, 128), c_chunk)

    def rows_of(h):
        return pl.ds(h * rows_half, rows_half)

    for h in range(halves):
        for j in range(n_row):
            primal[h, j] = p0_ref[rows_of(h), pl.ds(j * v_chunk, v_chunk)]
        for j in range(n_col):
            dual[h, j] = d0_ref[rows_of(h), pl.ds(j * c_chunk, c_chunk)]

    def spread(axis, me, count, k, src, dst, send, recv):
        return pltpu.make_async_remote_copy(
            src_ref=src,
            dst_ref=dst,
            send_sem=send,
            recv_sem=recv,
            device_id={axis: lax.rem(me + k, count)},
            device_id_type=MESH,
        )

    def adj_copy(h, k):
        dest = lax.rem(r + k, n_row)
        return spread(
            "row", r, n_row, k, adj_part.at[h, dest], adj_got.at[h, k],
            adj_send.at[h, k], adj_recv.at[h, k],
        )

    def pri_copy(h, k):
        return spread(
            "row", r, n_row, k, primal_new.at[h, r], primal_new.at[h, r],
            pri_send.at[h, k], pri_recv.at[h, k],
        )

    def fwd_copy(h, k):
        dest = lax.rem(c + k, n_col)
        return spread(
            "col", c, n_col, k, fwd_part.at[h, dest], fwd_got.at[h, k],
            fwd_send.at[h, k], fwd_recv.at[h, k],
        )

    def dua_copy(h, k):
        return spread(
            "col", c, n_col, k, dual.at[h, c], dual.at[h, c],
            dua_send.at[h, k], dua_recv.at[h, k],
        )

    def adjoint_start(h, first):
        if not first:
            for k in range(1, n_col):
                dua_copy(h, k).wait()
        for j in range(n_col):
            dual_low[h, :, j * c_chunk : (j + 1) * c_chunk] = dual[h, j].astype(jnp.bfloat16)
        for k in list(range(1, n_row)) + [0]:
            dest = lax.rem(r + k, n_row)
            adj_part[h, dest] = jnp.dot(
                dual_low[h], k_ref[dest], preferred_element_type=jnp.float32
            )
            if k:
                adj_copy(h, k).start()

    def primal_step(h):
        adjoint = adj_part[h, r]
        for k in range(1, n_row):
            adj_copy(h, k).wait()
            adjoint = adjoint + adj_got[h, k]
        primal_new[h, r] = jnp.minimum(
            jnp.maximum(primal[h, r] - PRIMAL_STEP * (obj_ref[:, v_own] - adjoint), 0.0),
            ub_ref[:, v_own],
        )
        for k in range(1, n_row):
            pri_copy(h, k).start()

    def forward_start(h):
        for k in range(1, n_row):
            pri_copy(h, k).wait()
        for j in range(n_row):
            new = primal_new[h, j]
            extrap_low[h, :, j * v_chunk : (j + 1) * v_chunk] = (
                2.0 * new - primal[h, j]
            ).astype(jnp.bfloat16)
            primal[h, j] = new
        for k in list(range(1, n_col)) + [0]:
            dest = lax.rem(c + k, n_col)
            fwd_part[h, dest] = jnp.dot(
                extrap_low[h], kt_ref[dest], preferred_element_type=jnp.float32
            )
            if k:
                fwd_copy(h, k).start()

    def dual_step(h):
        forward = fwd_part[h, c]
        for k in range(1, n_col):
            fwd_copy(h, k).wait()
            forward = forward + fwd_got[h, k]
        dual[h, c] = jnp.maximum(
            dual[h, c] + DUAL_STEP * (caps_ref[rows_of(h), c_own] - forward), 0.0
        )
        for k in range(1, n_col):
            dua_copy(h, k).start()

    row_blocks = c_chunk * n_col // block
    k_per, kt_per = v_chunk // block, c_chunk // block

    def transpose_rows(first, last):
        def one(i, carry):
            at = pl.multiple_of(i * block, block)
            into = pl.multiple_of(lax.rem(i, kt_per) * block, block)
            for j in range(n_row * k_per):
                inside = j % k_per * block
                kt_ref[lax.div(i, kt_per), j * block : (j + 1) * block, pl.ds(into, block)] = (
                    k_ref[j // k_per, pl.ds(at, block), inside : inside + block].T
                )
            return carry

        lax.fori_loop(first, last, one, 0)

    pl.semaphore_wait(barrier, n_row + n_col - 2)

    if halves == 1:
        adjoint_start(0, True)
        transpose_rows(0, row_blocks)
        primal_step(0)
        forward_start(0)
        dual_step(0)

        def body(_, carry):
            adjoint_start(0, False)
            primal_step(0)
            forward_start(0)
            dual_step(0)
            return carry

        lax.fori_loop(1, iters, body, 0)
    else:
        adjoint_start(0, True)
        transpose_rows(0, row_blocks // 2)
        primal_step(0)
        adjoint_start(1, True)
        transpose_rows(row_blocks // 2, row_blocks)
        forward_start(0)
        primal_step(1)
        dual_step(0)

        def body(_, carry):
            adjoint_start(0, False)
            forward_start(1)
            primal_step(0)
            dual_step(1)
            adjoint_start(1, False)
            forward_start(0)
            primal_step(1)
            dual_step(0)
            return carry

        lax.fori_loop(1, iters, body, 0)
        forward_start(1)
        dual_step(1)

    for h in range(halves):
        for j in range(n_row):
            p_out[rows_of(h), pl.ds(j * v_chunk, v_chunk)] = primal[h, j]
        for k in range(1, n_col):
            dua_copy(h, k).wait()
        for j in range(n_col):
            d_out[rows_of(h), pl.ds(j * c_chunk, c_chunk)] = dual[h, j]


def pdhg(block, n_col, dense, objective, upper_bound, power_caps, primal_start, dual_start):
    n_row, cons, v_chunk = dense.shape
    nvar, c_chunk = n_row * v_chunk, cons // n_col
    scenarios = primal_start.shape[0]
    halves = 2 if scenarios % 32 == 0 else 1
    rows_half = scenarios // halves
    vmem = pl.BlockSpec(memory_space=pltpu.VMEM)
    f32 = jnp.float32
    row_shape = (halves, n_row, rows_half, v_chunk)
    col_shape = (halves, n_col, rows_half, c_chunk)
    row_sem = pltpu.SemaphoreType.DMA((halves, n_row))
    col_sem = pltpu.SemaphoreType.DMA((halves, n_col))
    return pl.pallas_call(
        functools.partial(pdhg_kernel, ITERS, block),
        out_shape=(
            jax.ShapeDtypeStruct((scenarios, nvar), f32),
            jax.ShapeDtypeStruct((scenarios, cons), f32),
        ),
        in_specs=[vmem] * 6,
        out_specs=(vmem, vmem),
        scratch_shapes=[
            pltpu.VMEM((n_col, nvar, c_chunk), dense.dtype),
            pltpu.VMEM(row_shape, f32),
            pltpu.VMEM(row_shape, f32),
            pltpu.VMEM(col_shape, f32),
            pltpu.VMEM(row_shape, f32),
            pltpu.VMEM(row_shape, f32),
            pltpu.VMEM(col_shape, f32),
            pltpu.VMEM(col_shape, f32),
            pltpu.VMEM((halves, rows_half, nvar), jnp.bfloat16),
            pltpu.VMEM((halves, rows_half, cons), jnp.bfloat16),
            row_sem,
            row_sem,
            row_sem,
            row_sem,
            col_sem,
            col_sem,
            col_sem,
            col_sem,
        ],
        compiler_params=pltpu.CompilerParams(
            collective_id=0, has_side_effects=True, vmem_limit_bytes=40 << 20
        ),
        name="pdhg",
    )(
        dense,
        objective[None, :],
        upper_bound[None, :],
        power_caps,
        primal_start,
        dual_start,
    )


def pdhg_summed(dense, objective, upper_bound, power_caps, primal, dual):
    for _ in range(ITERS):
        part = jnp.dot(dual.astype(jnp.bfloat16), dense[0], preferred_element_type=jnp.float32)
        adjoint = lax.psum(part, "row")
        new = jnp.minimum(
            jnp.maximum(primal - PRIMAL_STEP * (objective[None, :] - adjoint), 0.0),
            upper_bound[None, :],
        )
        extrap = (2.0 * new - primal).astype(jnp.bfloat16)
        part = jnp.dot(extrap, dense[0].T, preferred_element_type=jnp.float32)
        forward = lax.psum(part, "col")
        dual = jnp.maximum(dual + DUAL_STEP * (power_caps - forward), 0.0)
        primal = new
    return primal, dual


def per_device(
    n_row,
    n_col,
    block_tiles,
    tile_row,
    tile_col,
    tile_count,
    objective,
    upper_bound,
    power_caps,
    primal_start,
    dual_start,
):
    block = block_tiles.shape[-1]
    cons = dual_start.shape[1]
    nvar = primal_start.shape[1]
    even = (nvar // block) % n_row == 0 and (cons // block) % n_col == 0
    dense = build_dense(
        block_tiles[0, 0],
        tile_row[0, 0],
        tile_col[0, 0],
        tile_count[0],
        cons,
        nvar,
        n_row if even else 1,
    )
    steps = functools.partial(pdhg, block, n_col) if even else pdhg_summed
    return steps(dense, objective, upper_bound, power_caps, primal_start, dual_start)


def solution(mesh):
    return jax.shard_map(
        functools.partial(per_device, mesh.shape["row"], mesh.shape["col"]),
        mesh=mesh,
        in_specs=(
            P(("groups", "row"), "col", None, None, None),
            P(("groups", "row"), "col", None),
            P(("groups", "row"), "col", None),
            P(("groups", "row"), "col"),
            P(("groups", "col")),
            P(("groups", "col")),
            P("groups", "row"),
            P("groups", "col"),
            P("groups", "row"),
        ),
        out_specs=(P("groups", "col"), P("groups", "row")),
        check_vma=False,
    )
```

```python
import functools

import jax
import jax.numpy as jnp
from jax import lax
from jax.experimental import pallas as pl
from jax.experimental.pallas import tpu as pltpu
from jax.sharding import PartitionSpec as P

ITERS = 6


PRIMAL_STEP = 0.5
DUAL_STEP = 0.2

TILE_STEP = 16
MESH = pl.DeviceIdType.MESH


def build_kernel(step_slots, rows_ref, cols_ref, count_ref, tiles_ref, k_ref):
    block = tiles_ref.shape[1]
    k_per = k_ref.shape[2] // block
    step = pl.program_id(0)

    @pl.when(step == 0)
    def _():
        k_ref[...] = jnp.zeros_like(k_ref)

    for i in range(step_slots):
        slot = step * step_slots + i

        @pl.when(slot < count_ref[0])
        def _():
            row = rows_ref[slot]
            col = cols_ref[slot]
            row_at = pl.multiple_of(row * block, block)
            k_in = pl.multiple_of(lax.rem(col, k_per) * block, block)
            k_ref[lax.div(col, k_per), pl.ds(row_at, block), pl.ds(k_in, block)] = tiles_ref[i]


def build_dense(tiles, rows, cols, count, cons, nvar, k_chunks):
    slots, block = tiles.shape[0], tiles.shape[1]
    step_slots = TILE_STEP if slots % TILE_STEP == 0 else 1
    k_shape = (k_chunks, cons, nvar // k_chunks)
    return pl.pallas_call(
        functools.partial(build_kernel, step_slots),
        out_shape=jax.ShapeDtypeStruct(k_shape, tiles.dtype),
        grid_spec=pltpu.PrefetchScalarGridSpec(
            num_scalar_prefetch=3,
            grid=(slots // step_slots,),
            in_specs=[pl.BlockSpec((step_slots, block, block), lambda t, *_: (t, 0, 0))],
            out_specs=pl.BlockSpec(k_shape, lambda t, *_: (0, 0, 0)),
        ),
        compiler_params=pltpu.CompilerParams(vmem_limit_bytes=40 << 20),
        name="build_dense",
    )(rows, cols, count, tiles)


def peer(me, k, count):
    if count & (count - 1):
        return lax.rem(me + k, count)
    for bit in range(count.bit_length() - 1):
        low = 1 << bit
        if k & low:
            me = me + low - 2 * low * lax.rem(lax.div(me, low), 2)
    return me


def pdhg_kernel(
    iters,
    block,
    k_ref,
    obj_ref,
    ub_ref,
    caps_ref,
    p0_ref,
    d0_ref,
    p_out,
    d_out,
    kt_ref,
    primal,
    primal_new,
    dual,
    adj_part,
    adj_got,
    fwd_part,
    fwd_got,
    extrap_low,
    dual_low,
    adj_send,
    adj_recv,
    pri_send,
    pri_recv,
    fwd_send,
    fwd_recv,
    dua_send,
    dua_recv,
):
    halves, n_row, rows_half, v_chunk = primal.shape
    _, n_col, _, c_chunk = dual.shape
    r = lax.axis_index("row")
    c = lax.axis_index("col")

    barrier = pltpu.get_barrier_semaphore()
    for k in range(1, n_row):
        pl.semaphore_signal(
            barrier, inc=1, device_id={"row": peer(r, k, n_row)}, device_id_type=MESH
        )
    for k in range(1, n_col):
        pl.semaphore_signal(
            barrier, inc=1, device_id={"col": peer(c, k, n_col)}, device_id_type=MESH
        )

    v_own = pl.ds(pl.multiple_of(r * v_chunk, 128), v_chunk)
    c_own = pl.ds(pl.multiple_of(c * c_chunk, 128), c_chunk)

    def rows_of(h):
        return pl.ds(h * rows_half, rows_half)

    for h in range(halves):
        for j in range(n_row):
            primal[h, j] = p0_ref[rows_of(h), pl.ds(j * v_chunk, v_chunk)]
        for j in range(n_col):
            dual[h, j] = d0_ref[rows_of(h), pl.ds(j * c_chunk, c_chunk)]

    def spread(axis, me, count, k, src, dst, send, recv):
        return pltpu.make_async_remote_copy(
            src_ref=src,
            dst_ref=dst,
            send_sem=send,
            recv_sem=recv,
            device_id={axis: peer(me, k, count)},
            device_id_type=MESH,
        )

    def adj_copy(h, k):
        dest = peer(r, k, n_row)
        return spread(
            "row", r, n_row, k, adj_part.at[h, dest], adj_got.at[h, k],
            adj_send.at[h, k], adj_recv.at[h, k],
        )

    def pri_copy(h, k):
        return spread(
            "row", r, n_row, k, primal_new.at[h, r], primal_new.at[h, r],
            pri_send.at[h, k], pri_recv.at[h, k],
        )

    def fwd_copy(h, k):
        dest = peer(c, k, n_col)
        return spread(
            "col", c, n_col, k, fwd_part.at[h, dest], fwd_got.at[h, k],
            fwd_send.at[h, k], fwd_recv.at[h, k],
        )

    def dua_copy(h, k):
        return spread(
            "col", c, n_col, k, dual.at[h, c], dual.at[h, c],
            dua_send.at[h, k], dua_recv.at[h, k],
        )

    def adjoint_start(h, first):
        if not first:
            for k in range(1, n_col):
                dua_copy(h, k).wait()
        for j in range(n_col):
            dual_low[h, :, j * c_chunk : (j + 1) * c_chunk] = dual[h, j].astype(jnp.bfloat16)
        for k in range(n_row - 1, -1, -1):
            dest = peer(r, k, n_row)
            adj_part[h, dest] = jnp.dot(
                dual_low[h], k_ref[dest], preferred_element_type=jnp.float32
            )
            if k:
                adj_copy(h, k).start()

    def primal_step(h):
        adjoint = adj_part[h, r]
        for k in range(1, n_row):
            adj_copy(h, k).wait()
            adjoint = adjoint + adj_got[h, k]
        primal_new[h, r] = jnp.minimum(
            jnp.maximum(primal[h, r] - PRIMAL_STEP * (obj_ref[:, v_own] - adjoint), 0.0),
            ub_ref[:, v_own],
        )
        for k in range(n_row - 1, 0, -1):
            pri_copy(h, k).start()

    def forward_start(h):
        for k in range(1, n_row):
            pri_copy(h, k).wait()
        for j in range(n_row):
            new = primal_new[h, j]
            extrap_low[h, :, j * v_chunk : (j + 1) * v_chunk] = (
                2.0 * new - primal[h, j]
            ).astype(jnp.bfloat16)
            primal[h, j] = new
        for k in range(n_col - 1, -1, -1):
            dest = peer(c, k, n_col)
            fwd_part[h, dest] = jnp.dot(
                extrap_low[h], kt_ref[dest], preferred_element_type=jnp.float32
            )
            if k:
                fwd_copy(h, k).start()

    def dual_step(h):
        forward = fwd_part[h, c]
        for k in range(1, n_col):
            fwd_copy(h, k).wait()
            forward = forward + fwd_got[h, k]
        dual[h, c] = jnp.maximum(
            dual[h, c] + DUAL_STEP * (caps_ref[rows_of(h), c_own] - forward), 0.0
        )
        for k in range(n_col - 1, 0, -1):
            dua_copy(h, k).start()

    row_blocks = c_chunk * n_col // block
    k_per, kt_per = v_chunk // block, c_chunk // block

    def transpose_rows(first, last):
        def one(i, carry):
            at = pl.multiple_of(i * block, block)
            into = pl.multiple_of(lax.rem(i, kt_per) * block, block)
            for j in range(n_row * k_per):
                inside = j % k_per * block
                kt_ref[lax.div(i, kt_per), j * block : (j + 1) * block, pl.ds(into, block)] = (
                    k_ref[j // k_per, pl.ds(at, block), inside : inside + block].T
                )
            return carry

        lax.fori_loop(first, last, one, 0)

    pl.semaphore_wait(barrier, n_row + n_col - 2)

    if halves == 1:
        adjoint_start(0, True)
        transpose_rows(0, row_blocks)
        primal_step(0)
        forward_start(0)
        dual_step(0)

        def body(_, carry):
            adjoint_start(0, False)
            primal_step(0)
            forward_start(0)
            dual_step(0)
            return carry

        lax.fori_loop(1, iters, body, 0)
    else:
        adjoint_start(0, True)
        transpose_rows(0, row_blocks // 2)
        primal_step(0)
        adjoint_start(1, True)
        transpose_rows(row_blocks // 2, row_blocks)
        forward_start(0)
        primal_step(1)
        dual_step(0)

        def body(_, carry):
            adjoint_start(0, False)
            forward_start(1)
            primal_step(0)
            dual_step(1)
            adjoint_start(1, False)
            forward_start(0)
            primal_step(1)
            dual_step(0)
            return carry

        lax.fori_loop(1, iters, body, 0)
        forward_start(1)
        dual_step(1)

    for h in range(halves):
        for j in range(n_row):
            p_out[rows_of(h), pl.ds(j * v_chunk, v_chunk)] = primal[h, j]
        for k in range(1, n_col):
            dua_copy(h, k).wait()
        for j in range(n_col):
            d_out[rows_of(h), pl.ds(j * c_chunk, c_chunk)] = dual[h, j]


def pdhg(block, n_col, dense, objective, upper_bound, power_caps, primal_start, dual_start):
    n_row, cons, v_chunk = dense.shape
    nvar, c_chunk = n_row * v_chunk, cons // n_col
    scenarios = primal_start.shape[0]
    halves = 2 if scenarios % 32 == 0 else 1
    rows_half = scenarios // halves
    vmem = pl.BlockSpec(memory_space=pltpu.VMEM)
    f32 = jnp.float32
    row_shape = (halves, n_row, rows_half, v_chunk)
    col_shape = (halves, n_col, rows_half, c_chunk)
    row_sem = pltpu.SemaphoreType.DMA((halves, n_row))
    col_sem = pltpu.SemaphoreType.DMA((halves, n_col))
    return pl.pallas_call(
        functools.partial(pdhg_kernel, ITERS, block),
        out_shape=(
            jax.ShapeDtypeStruct((scenarios, nvar), f32),
            jax.ShapeDtypeStruct((scenarios, cons), f32),
        ),
        in_specs=[vmem] * 6,
        out_specs=(vmem, vmem),
        scratch_shapes=[
            pltpu.VMEM((n_col, nvar, c_chunk), dense.dtype),
            pltpu.VMEM(row_shape, f32),
            pltpu.VMEM(row_shape, f32),
            pltpu.VMEM(col_shape, f32),
            pltpu.VMEM(row_shape, f32),
            pltpu.VMEM(row_shape, f32),
            pltpu.VMEM(col_shape, f32),
            pltpu.VMEM(col_shape, f32),
            pltpu.VMEM((halves, rows_half, nvar), jnp.bfloat16),
            pltpu.VMEM((halves, rows_half, cons), jnp.bfloat16),
            row_sem,
            row_sem,
            row_sem,
            row_sem,
            col_sem,
            col_sem,
            col_sem,
            col_sem,
        ],
        compiler_params=pltpu.CompilerParams(
            collective_id=0, has_side_effects=True, vmem_limit_bytes=40 << 20
        ),
        name="pdhg",
    )(
        dense,
        objective[None, :],
        upper_bound[None, :],
        power_caps,
        primal_start,
        dual_start,
    )


def pdhg_summed(dense, objective, upper_bound, power_caps, primal, dual):
    for _ in range(ITERS):
        part = jnp.dot(dual.astype(jnp.bfloat16), dense[0], preferred_element_type=jnp.float32)
        adjoint = lax.psum(part, "row")
        new = jnp.minimum(
            jnp.maximum(primal - PRIMAL_STEP * (objective[None, :] - adjoint), 0.0),
            upper_bound[None, :],
        )
        extrap = (2.0 * new - primal).astype(jnp.bfloat16)
        part = jnp.dot(extrap, dense[0].T, preferred_element_type=jnp.float32)
        forward = lax.psum(part, "col")
        dual = jnp.maximum(dual + DUAL_STEP * (power_caps - forward), 0.0)
        primal = new
    return primal, dual


def per_device(
    n_row,
    n_col,
    block_tiles,
    tile_row,
    tile_col,
    tile_count,
    objective,
    upper_bound,
    power_caps,
    primal_start,
    dual_start,
):
    block = block_tiles.shape[-1]
    cons = dual_start.shape[1]
    nvar = primal_start.shape[1]
    even = (nvar // block) % n_row == 0 and (cons // block) % n_col == 0
    dense = build_dense(
        block_tiles[0, 0],
        tile_row[0, 0],
        tile_col[0, 0],
        tile_count[0],
        cons,
        nvar,
        n_row if even else 1,
    )
    steps = functools.partial(pdhg, block, n_col) if even else pdhg_summed
    return steps(dense, objective, upper_bound, power_caps, primal_start, dual_start)


def solution(mesh):
    return jax.shard_map(
        functools.partial(per_device, mesh.shape["row"], mesh.shape["col"]),
        mesh=mesh,
        in_specs=(
            P(("groups", "row"), "col", None, None, None),
            P(("groups", "row"), "col", None),
            P(("groups", "row"), "col", None),
            P(("groups", "row"), "col"),
            P(("groups", "col")),
            P(("groups", "col")),
            P("groups", "row"),
            P("groups", "col"),
            P("groups", "row"),
        ),
        out_specs=(P("groups", "col"), P("groups", "row")),
        check_vma=False,
    )
```
